32 devices in a mesh: prow: 4 (over z), pcol: 8 (over y, x, core).
Axes of the slice: x: 2, y: 2, z: 4, core: 2. Of those that a mesh axis runs over, the one named last changes fastest.
Arguments:
- matrix: float32 [6, 4, 256, 3, 8, 256], P(None, 'prow', None, None, 'pcol'), may hold values from -6 to 6
- row_order: int32 [6144], replicated, may hold values from 0 to 6143, as said below
- inverses: float32 [4, 256, 256], replicated, may hold values from -0.0234375 to 0.0234375
- lower_fill: int32 [4, 24], replicated, may hold values 0 or 1
- upper_fill: int32 [4, 24], replicated, may hold values 0 or 1
Outputs:
- factored: float32 [6, 4, 256, 3, 8, 256], P(None, 'prow', None, None, 'pcol')
The draws below stay inside these ranges and needn't reach their ends.
Inputs may be any that keep to these rules, and one draw needn't show every extreme that they name: row_order is a permutation of the rows; of the rows whose block row index is congruent to p modulo the number of indices of prow, exactly 6 * 256 divided by that number go to rows whose block row index is congruent to s, for every p and s.
All inputs are finite; a program needn't handle non-finite values.
Results may differ from the reference program's by a relative error of at most 0.0002.
Values sent between devices are 32-bit elements; how exact they have to be, the bound alone decides.
A program may use at most 128 MiB of HBM per device.

```python
import jax
import jax.numpy as jnp
from jax import lax

B = 256
CB = 3
PANELS = 4
RB = 6
NB = 24
N_PROW = 4
N_PCOL = 8


def draw_row_order(key, part):
    local_rows = RB * B
    share = local_rows // N_PROW
    offsets = jnp.arange(local_rows, dtype=jnp.int32)
    owners = jnp.arange(N_PROW, dtype=jnp.int32)
    rows = (offsets[None, :] // B * N_PROW + owners[:, None]) * B + offsets[None, :] % B
    first, second = jax.random.split(jax.random.fold_in(key, 11))

    def shuffle(subkey):
        return jax.vmap(lambda single: jax.random.permutation(single, local_rows))(jax.random.split(subkey, N_PROW))
    sources = jnp.take_along_axis(rows, shuffle(first), 1).reshape(N_PROW, N_PROW, share)
    targets = jnp.take_along_axis(rows, shuffle(second), 1).reshape(N_PROW, N_PROW, share)
    moved = jnp.transpose(targets, (1, 0, 2)).reshape(-1)
    return jnp.zeros((NB * B,), jnp.int32).at[sources.reshape(-1)].set(moved)


def set_ends(values, stream_key, least, top_value):
    dims = values.shape
    place = [jax.random.randint(jax.random.fold_in(stream_key, axis), (), 0, dims[axis]) for axis in range(len(dims))]
    values = values.at[tuple(place)].set(least)
    longest = dims.index(max(dims))
    place[longest] = (place[longest] + 1) % dims[longest]
    return values.at[tuple(place)].set(top_value)


def shard_levels(rng, extent, cuts, least, top_value):
    level, own = 1.0, jax.random.fold_in(rng, 6)
    for position, shards_of in cuts:
        steps = jnp.exp(jax.random.uniform(jax.random.fold_in(own, position), (shards_of,), jnp.float32, least / len(cuts), top_value / len(cuts)))
        level = level * jnp.repeat(steps, extent[position] // shards_of).reshape([-1 if axis == position else 1 for axis in range(len(extent))])
    return level


def bell_draw(own_key, shape, spread, reach, pieces=(), kind=jnp.bfloat16):
    factor_of = shard_levels(own_key, shape, pieces, -0.22, 0.18) if pieces else 1.0
    entries = jax.random.normal(own_key, shape, jnp.float32) * spread * factor_of
    return jnp.minimum(jnp.maximum(entries, -reach), reach).astype(kind)


def setup_inputs(seed: int = 0) -> dict:
    streams_of = jax.random.split(jax.random.key(seed), 6)
    matrix = bell_draw(streams_of[0], (RB, N_PROW, B, CB, N_PCOL, B), 1.0, 6.0, ((1, 4), (4, 8)), jnp.float32)
    row_order = draw_row_order(jax.random.fold_in(streams_of[5], 71), 0)
    inverses = bell_draw(streams_of[2], (PANELS, B, B), (B * B) ** -0.5, 0.0234375, (), jnp.float32)
    lower_fill = set_ends((jax.random.randint(streams_of[3], (PANELS, NB), 0, 4) < 3).astype(jnp.int32), jax.random.fold_in(streams_of[3], 1), 0, 1)
    upper_fill = set_ends((jax.random.randint(streams_of[4], (PANELS, NB), 0, 4) < 3).astype(jnp.int32), jax.random.fold_in(streams_of[4], 1), 0, 1)
    return dict(matrix=matrix, row_order=row_order, inverses=inverses, lower_fill=lower_fill, upper_fill=upper_fill)


def reference(matrix, row_order, inverses, lower_fill, upper_fill):
    order_n = NB * B
    whole = matrix.reshape(order_n, order_n)
    work = jnp.zeros_like(whole).at[row_order].set(whole)
    blocks = jnp.arange(NB, dtype=jnp.int32)
    for k in range(PANELS):
        keep_rows = jnp.repeat(((blocks > k) & (lower_fill[k] == 1)).astype(jnp.float32), B)
        keep_cols = jnp.repeat(((blocks > k) & (upper_fill[k] == 1)).astype(jnp.float32), B)
        column = work[:, k * B:(k + 1) * B]
        lower = jnp.dot(column, inverses[k], precision=lax.Precision.HIGHEST, preferred_element_type=jnp.float32) * keep_rows[:, None]
        upper = work[k * B:(k + 1) * B, :] * keep_cols[None, :]
        start = (k + 1) * B
        update = jnp.dot(lower[start:], upper[:, start:], precision=lax.Precision.HIGHEST, preferred_element_type=jnp.float32)
        work = work.at[start:, start:].add(-update)
        work = work.at[start:, k * B:(k + 1) * B].set(lower[start:])
    return work.reshape(RB, N_PROW, B, CB, N_PCOL, B)
```

```python
import functools

import jax
import jax.numpy as jnp
from jax import lax
from jax.experimental import pallas as pl
from jax.experimental.pallas import tpu as pltpu
from jax.sharding import PartitionSpec as P


def mm(a, b):
    return jnp.dot(a, b, precision=lax.Precision.HIGH, preferred_element_type=jnp.float32)


def index_lists(row_order, rows, width, prows, here_row):
    local_rows = rows * width
    blocks = row_order.reshape(rows, prows, width)
    targets = lax.dynamic_index_in_dim(blocks, here_row, 1, keepdims=False).reshape(-1)
    local = jnp.arange(local_rows, dtype=jnp.int32)
    sending = (targets // width % prows) * local_rows + local
    by_source = jnp.transpose(blocks, (1, 0, 2)).reshape(-1)
    dest_local = by_source // width // prows * width + by_source % width
    mine = by_source // width % prows == here_row
    position = jnp.cumsum(mine.astype(jnp.int32)) - 1
    key = jnp.where(mine, dest_local * local_rows + position, local_rows * local_rows)
    both = jnp.concatenate([sending, prows * local_rows + key])
    both = lax.sort(both, is_stable=False)[: 2 * local_rows] % local_rows
    return both[:local_rows], both[local_rows:]


def keep_of(fill_row, panel, blocks):
    return (blocks > panel) & (fill_row[blocks] == 1)


def body(matrix, row_order, inverses, lower_fill, upper_fill):
    nrows = matrix.shape[0]
    width = matrix.shape[2]
    ncols = matrix.shape[3]
    prows = lax.axis_size("prow")
    pcols = lax.axis_size("pcol")
    p = lax.axis_index("prow")
    q = lax.axis_index("pcol")
    panels = inverses.shape[0]
    local_rows = nrows * width
    cols = ncols * width
    sending, taking = index_lists(row_order, nrows, width, prows, p)
    work = matrix.reshape(local_rows, cols)
    outgoing = work[sending].reshape(prows, local_rows // prows, cols)
    incoming = lax.all_to_all(outgoing, "prow", split_axis=0, concat_axis=0, tiled=True)
    work = incoming.reshape(local_rows, cols)[taking]
    tops = lax.all_gather(work[:width], "prow", axis=0, tiled=False)[:panels]
    tops = tops.reshape(panels * width, cols)
    column = jnp.concatenate([tops[:, :width], work[:, :width]], axis=0)
    ratio = pcols // panels
    pieces = column.reshape(ratio, -1, width)
    piece = jnp.where(q < panels, pieces[0], 0.0)
    for j in range(1, ratio):
        pairs = [(k, k + panels * j) for k in range(panels)]
        piece = piece + lax.ppermute(pieces[j], "pcol", pairs)
    every = lax.all_gather(piece, "pcol", axis=0, tiled=False)
    every = every.reshape(ratio, panels, piece.shape[0], width)
    columns = [every[:, k].reshape(column.shape) for k in range(panels)]
    row_blocks = jnp.concatenate(
        [jnp.arange(panels, dtype=jnp.int32), jnp.arange(nrows, dtype=jnp.int32) * prows + p]
    )
    col_blocks = jnp.arange(ncols, dtype=jnp.int32) * pcols + q
    corner = panels * width
    lowers, uppers = [], []
    mine = work[:, :width]
    for k in range(panels):
        here = columns[k]
        for m in range(k):
            keep = (upper_fill[m, k] == 1).astype(jnp.float32)
            part = here[m * width : (m + 1) * width] * keep
            here = here - mm(lowers[m], part)
        columns[k] = here
        row_keep = jnp.repeat(keep_of(lower_fill[k], k, row_blocks), width)[:, None]
        lower = jnp.where(row_keep, mm(here, inverses[k]), 0.0)
        lowers.append(lower)
        row = tops[k * width : (k + 1) * width]
        for m in range(k):
            row = row - mm(lower_rows(lowers[m], k, width), uppers[m])
        col_keep = jnp.repeat(keep_of(upper_fill[k], k, col_blocks), width)[None, :]
        uppers.append(jnp.where(col_keep, row, 0.0))
    left = jnp.concatenate([x[corner:] for x in lowers], axis=1)
    out = work - mm(left, jnp.concatenate(uppers, axis=0))
    row_ids = jnp.repeat(row_blocks[panels:], width)[:, None]
    first = out[:, :width]
    for k in range(panels):
        first = jnp.where((q == k) & (row_ids > k), lowers[k][corner:], first)
    out = out.at[:, :width].set(first)
    return out.reshape(nrows, 1, width, ncols, 1, width)


def lower_rows(lower, k, width):
    return lower[k * width : (k + 1) * width]


MESH = pl.DeviceIdType.MESH


def tables(row_order, rows, width, here_row):
    local_rows = rows * width
    share = local_rows // 4
    blocks = row_order.reshape(rows, 4, width)
    targets = lax.dynamic_index_in_dim(blocks, here_row, 1, keepdims=False).reshape(-1)
    local = jnp.arange(local_rows, dtype=jnp.int32)
    late = (targets >= 4 * width).astype(jnp.int32)
    sending = (targets // width % 4 * 2 + late) * local_rows + local
    by_source = jnp.transpose(blocks, (1, 0, 2)).reshape(4, local_rows)
    mine = by_source // width % 4 == here_row
    first = mine & (by_source < 4 * width)
    firsts = jnp.cumsum(first.astype(jnp.int32), axis=1)
    lates = jnp.cumsum((mine & ~first).astype(jnp.int32), axis=1)
    rank = jnp.where(first, firsts, firsts[:, -1:] + lates) - 1
    position = jnp.arange(4, dtype=jnp.int32)[:, None] * share + rank
    dest_local = by_source // width // 4 * width + by_source % width
    key = jnp.where(mine, dest_local * local_rows + position, local_rows * local_rows)
    both = jnp.concatenate([sending, 8 * local_rows + key.reshape(-1)])
    both = lax.sort(both, is_stable=False)[: 2 * local_rows] % local_rows
    taking = both[local_rows:]
    head = taking[:width]
    return both[:local_rows], taking, head // share * width + head % share


def halves(x):
    high = x.astype(jnp.bfloat16)
    return high, (x - high.astype(jnp.float32)).astype(jnp.bfloat16)


def dot3(a, b):
    def dot(x, y):
        return jnp.dot(x, y, preferred_element_type=jnp.float32)

    return dot(a[0], b[0]) + dot(a[0], b[1]) + dot(a[1], b[0])


def fused_kernel(
    nrows, width, sending, taking, heads, lower_fill, upper_fill, mat_in, inv, out,
    mat, send, early0, early1, early2, all0, all1, all2, work, tops, cols,
    lh, ll, uh, ul, ch, cl, ih, il,
    a2a_send, a2a_recv, g_send, g_recv, x_send, x_recv, y_send, y_recv, s_send, s_recv,
    keep_sem, join_sem, mat_sem,
):
    p = lax.axis_index("prow")
    q = lax.axis_index("pcol")
    side, across, core = q // 4, q // 2 % 2, q % 2
    xq = side * 4 + (1 - across) * 2 + core
    yq = (1 - side) * 4 + across * 2 + core
    sq = side * 4 + across * 2 + (1 - core)
    local_rows = nrows * width
    share = local_rows // 4
    top = 2 * width
    size = 4 * width
    span6 = 6 * width
    late = 2 * (share - width)
    partner = p + 1 - 2 * (p % 2)
    others = [((p + 2) % 4, q), (3 - p, q), (partner, q)]
    early = (early0, early1, early2)
    full = (all0, all1, all2)

    load = pltpu.make_async_copy(mat_in, mat, mat_sem.at[6])
    load.start()
    barrier = pltpu.get_barrier_semaphore()
    for peer in others + [(p, xq), (p, yq), (p, sq)]:
        pl.semaphore_signal(barrier, inc=1, device_id=peer, device_id_type=MESH)
    pl.semaphore_wait(barrier, 6)
    load.wait()

    def remote(src, dst, send_sem, recv_sem, peer):
        return pltpu.make_async_remote_copy(
            src_ref=src, dst_ref=dst, send_sem=send_sem, recv_sem=recv_sem,
            device_id=peer, device_id_type=MESH,
        )

    def pick(dst, index, index_base, source, pitch, offset, count):
        unroll = 8

        def group(g, carry):
            for u in range(unroll):
                row = index[index_base + g * unroll + u]
                dst[pl.ds(g * (2 * unroll) + 2 * u, 2), :] = source[
                    pl.ds(row * pitch + offset, 2), :
                ]
            return carry

        lax.fori_loop(0, count // unroll, group, 0)

    def a2a(c, slot, part):
        if part == 0:
            src = send.at[c, slot, pl.ds(0, top)]
            dst = early[c].at[pl.ds(pl.multiple_of(p * top, 8), top)]
        else:
            src = send.at[c, slot, pl.ds(top, late)]
            dst = full[c].at[pl.ds(pl.multiple_of(p * (2 * share) + top, 8), late)]
        return remote(
            src, dst, a2a_send.at[c, slot, part], a2a_recv.at[c, slot, part], others[slot]
        )

    def pick_send(c, slot, part):
        base = others[slot][0] * share
        if part == 0:
            pick(send.at[c, slot, pl.ds(0, top)], sending, base, mat, 6, 2 * c, width)
        else:
            pick(
                send.at[c, slot, pl.ds(top, late)], sending, base + width, mat, 6, 2 * c,
                share - width,
            )

    def pick_mine(c):
        here = early[c].at[pl.ds(pl.multiple_of(p * top, 8), top)]
        pick(here, sending, p * share, mat, 6, 2 * c, width)
        here = full[c].at[pl.ds(pl.multiple_of(p * (2 * share) + top, 8), late)]
        pick(here, sending, p * share + width, mat, 6, 2 * c, share - width)

    def start(c, slots, part):
        for slot in slots:
            a2a(c, slot, part).start()

    def join(c, s):
        return pltpu.make_async_copy(
            early[c].at[pl.ds(s * top, top)], full[c].at[pl.ds(s * 2 * share, top)],
            join_sem.at[c, s],
        )

    def top_of(c, owner):
        return tops.at[c, pl.ds(pl.multiple_of(owner * top, 8), top)]

    def early_in(c):
        for slot in range(3):
            a2a(c, slot, 0).wait_recv()
        for s in range(4):
            join(c, s).start()
        pick(top_of(c, p), heads, 0, early[c], 2, 0, width)

    def late_in(c):
        for slot in range(3):
            a2a(c, slot, 1).wait_recv()
        for s in range(4):
            join(c, s).wait()

    cross = (2 - p // 2, q)
    inner = (p == 1) | (p == 2)
    outer = (p == 0) | (p == 3)
    far = 2 - 2 * (p // 2)

    def gather_copy(c, owner, sem, peer):
        here = top_of(c, owner)
        return remote(here, here, g_send.at[c, sem], g_recv.at[c, owner], peer)

    def gather_start(c):
        gather_copy(c, p, 1, cross).start()
        gather_copy(c, p, 0, (partner, q)).start()

    def gather_relay(c):
        @pl.when(inner)
        def _():
            for j in range(2):
                gather_copy(c, far + j, 2 + j, (partner, q)).wait_recv()
                gather_copy(c, far + j, 2 + j, (partner, q)).start()

    def gather_end(c):
        gather_copy(c, partner, 0, (partner, q)).wait_recv()

        @pl.when(outer)
        def _():
            for j in range(2):
                gather_copy(c, far + j, 2 + j, (partner, q)).wait_recv()

    def gather_sent(c):
        gather_copy(c, p, 1, cross).wait_send()
        gather_copy(c, p, 0, (partner, q)).wait_send()

        @pl.when(inner)
        def _():
            for j in range(2):
                gather_copy(c, far + j, 2 + j, (partner, q)).wait_send()

    straight = across * 2 + core
    crossed = (1 - across) * 2 + core
    spots = [4 * top + 0, 4 * top + size, 4 * top + 2 * size, 0, size]

    def place(block, piece):
        return cols.at[block, pl.ds(spots[piece], size)]

    def first_source(piece):
        if piece < 3:
            return work.at[pl.ds(piece * size, size)]
        return tops.at[0, pl.ds((piece - 3) * size, size)]

    def to_x(src, piece):
        return remote(src, place(straight, piece), x_send.at[piece], x_recv.at[piece], (p, xq))

    def to_y(src, piece):
        return remote(src, place(straight, piece), y_send.at[piece], y_recv.at[piece], (p, yq))

    def to_s(src, kind, piece):
        block = (straight, crossed)[kind]
        return remote(
            src, place(block, piece), s_send.at[kind, piece], s_recv.at[kind, piece], (p, sq)
        )

    def keep_own(piece):
        return pltpu.make_async_copy(
            first_source(piece), place(straight, piece), keep_sem.at[piece]
        )

    def column_start(piece):
        @pl.when(side == 0)
        def _():
            src = first_source(piece)
            to_y(src, piece).start()
            to_x(src, piece).start()
            to_s(src, 0, piece).start()
            keep_own(piece).start()

    def column_pass(piece):
        @pl.when(side == 1)
        def _():
            here = place(straight, piece)
            to_y(here, piece).wait_recv()
            to_x(here, piece).start()
            to_s(here, 0, piece).start()

    def column_across(piece):
        here = place(crossed, piece)
        remote(here, here, x_send.at[piece], x_recv.at[piece], (p, xq)).wait_recv()
        to_s(here, 1, piece).start()

    def column_ready(piece):
        for kind in range(2):
            block = (straight, crossed)[kind]
            theirs = place(block + 1 - 2 * core, piece)
            remote(
                theirs, theirs, s_send.at[kind, piece], s_recv.at[kind, piece], (p, sq)
            ).wait_recv()

        @pl.when(side == 0)
        def _():
            keep_own(piece).wait()

    def column_sent(piece):
        for kind in range(2):
            block = (straight, crossed)[kind]
            to_s(place(block, piece), kind, piece).wait_send()
        to_x(place(straight, piece), piece).wait_send()

        @pl.when(side == 0)
        def _():
            to_y(place(straight, piece), piece).wait_send()

    def kept(fill, k, block):
        return jnp.where((block > k) & (fill[k, block] == 1), 1.0, 0.0)

    def column_tile(k, start):
        left = cols[k, pl.ds(2 * start, width, stride=2), :]
        right = cols[k, pl.ds(2 * start + 1, width, stride=2), :]
        return jnp.concatenate([left, right], axis=1)

    def lower_of(start, deep):
        rows = pl.ds(start, width)
        return lh[rows, :deep], ll[rows, :deep]

    def put_lower(start, k, h, keep):
        rows, here = pl.ds(start, width), slice(k * width, (k + 1) * width)
        inverse = ih[here, :], il[here, :]
        lh[rows, here], ll[rows, here] = halves(dot3(halves(h), inverse) * keep)

    def corner():
        for r in range(4):
            for k in range(4):
                if k == r:
                    continue
                h = column_tile(k, r * width)
                deep = min(r, k) * width
                if deep:
                    h = h - dot3(lower_of(r * width, deep), (ch[k, :deep, :], cl[k, :deep, :]))
                if k < r:
                    put_lower(r * width, k, h, kept(lower_fill, k, r))
                else:
                    here = slice(r * width, (r + 1) * width)
                    ch[k, here, :], cl[k, here, :] = halves(h * kept(upper_fill, r, k))

    def panels(piece):
        for k in range(4):
            for i in (2 * piece, 2 * piece + 1):
                begin = (4 + i) * width
                h = column_tile(k, begin)
                deep = k * width
                if deep:
                    h = h - dot3(lower_of(begin, deep), (ch[k, :deep, :], cl[k, :deep, :]))
                put_lower(begin, k, h, kept(lower_fill, k, i * 4 + p))

    def upper(c):
        span = slice(c * width, (c + 1) * width)
        for r in range(4):
            left = tops[c, pl.ds(2 * r * width, width, stride=2), :]
            right = tops[c, pl.ds(2 * r * width + 1, width, stride=2), :]
            u = jnp.concatenate([left, right], axis=1)
            deep = r * width
            if deep:
                u = u - dot3(lower_of(r * width, deep), (uh[:deep, span], ul[:deep, span]))
            here = slice(r * width, (r + 1) * width)
            uh[here, span], ul[here, span] = halves(u * kept(upper_fill, r, c * 8 + q))

    def update(c):
        span = slice(c * width, (c + 1) * width)

        def tile(i, carry):
            begin = pl.multiple_of((4 + i) * width, width)
            value = dot3(lower_of(begin, 4 * width), (uh[:, span], ul[:, span]))
            if c == 0:
                at = pl.multiple_of(i * (2 * width), 8)
                old = jnp.concatenate(
                    [
                        work[pl.ds(at, width, stride=2), :],
                        work[pl.ds(at + 1, width, stride=2), :],
                    ],
                    axis=1,
                )
                value = old - value
                for k in range(4):
                    here = slice(k * width, (k + 1) * width)
                    rows = pl.ds(begin, width)
                    low = lh[rows, here].astype(jnp.float32) + ll[rows, here].astype(jnp.float32)
                    value = jnp.where((q == k) & (i * 4 + p > k), low, value)
            for half in range(2):
                part = value[:, half * 128 : (half + 1) * 128]
                rows = pl.ds(i * span6 + 2 * c + half, width, stride=6)
                if c == 1:
                    part = mat[rows, :] - part
                mat[rows, :] = part
            return carry

        lax.fori_loop(0, nrows, tile, 0)

    def take(c, subtract, first, count):
        def group(g, carry):
            for u in range(8):
                row = taking[first + g * 8 + u]
                value = full[c][pl.ds(row * 2, 2), :]
                here = pl.ds((first + g * 8) * 6 + u * 6 + 2 * c, 2)
                if subtract:
                    value = value - mat[here, :]
                mat[here, :] = value
            return carry

        lax.fori_loop(0, count // 8, group, 0)

    for slot in range(3):
        pick_send(0, slot, 0)
        start(0, (slot,), 0)
    for slot in range(3):
        pick_send(0, slot, 1)
        start(0, (slot,), 1)
    pick_mine(0)
    for c in (1, 2):
        for part in range(2):
            for slot in range(3):
                pick_send(c, slot, part)
        pick_mine(c)
    ih[...], il[...] = halves(inv[...])
    early_in(0)
    gather_start(0)
    start(1, (0, 1, 2), 0)
    late_in(0)
    pick(work, taking, 0, all0, 2, 0, local_rows)
    column_start(0)
    gather_relay(0)
    start(1, (0, 1, 2), 1)
    gather_end(0)
    column_start(3)
    column_start(4)
    column_start(1)
    column_start(2)
    column_pass(0)
    column_across(0)
    column_pass(3)
    column_across(3)
    early_in(1)
    gather_start(1)
    start(2, (0, 1, 2), 0)
    start(2, (0,), 1)
    column_pass(4)
    column_across(4)
    late_in(1)
    take(1, False, 0, local_rows)
    gather_relay(1)
    column_pass(1)
    column_ready(3)
    column_ready(4)
    corner()
    column_across(1)
    column_pass(2)
    column_ready(0)
    panels(0)
    column_across(2)
    gather_end(1)
    column_ready(1)
    panels(1)
    early_in(2)
    gather_start(2)
    start(2, (1, 2), 1)
    upper(0)
    upper(1)
    column_ready(2)
    panels(2)
    gather_relay(2)
    update(0)
    update(1)
    gather_end(2)
    upper(2)
    update(2)
    late_in(2)

    def leave(i):
        rows = pl.ds(i * span6, span6)
        return pltpu.make_async_copy(mat.at[rows], out.at[rows], mat_sem.at[i])

    for i in range(nrows):
        take(2, True, i * width, width)
        leave(i).start()
    for c in range(3):
        gather_sent(c)
        for slot in range(3):
            for part in range(2):
                a2a(c, slot, part).wait_send()
    for piece in range(5):
        column_sent(piece)
    for i in range(nrows):
        leave(i).wait()


def fused(matrix, sending, taking, heads, lower_fill, upper_fill, inverses, nrows, width):
    local_rows = nrows * width
    share = local_rows // 4
    dma = pltpu.SemaphoreType.DMA
    vmem = pl.BlockSpec(memory_space=pltpu.VMEM)
    smem = pl.BlockSpec(memory_space=pltpu.SMEM)
    hbm = pl.BlockSpec(memory_space=pl.ANY)
    f32, bf16 = jnp.float32, jnp.bfloat16
    rows = (4 + nrows) * width
    return pl.pallas_call(
        functools.partial(fused_kernel, nrows, width),
        out_shape=jax.ShapeDtypeStruct((6 * local_rows, 128), f32),
        in_specs=[smem] * 5 + [hbm, vmem],
        out_specs=hbm,
        scratch_shapes=[
            pltpu.VMEM((6 * local_rows, 128), f32),
            pltpu.VMEM((3, 3, 2 * share, 128), f32),
            *[pltpu.VMEM((8 * width, 128), f32)] * 3,
            *[pltpu.VMEM((2 * local_rows, 128), f32)] * 3,
            pltpu.VMEM((2 * local_rows, 128), f32),
            pltpu.VMEM((3, 8 * width, 128), f32),
            pltpu.VMEM((4, 8 * width + 2 * local_rows, 128), f32),
            *[pltpu.VMEM((rows, 4 * width), bf16)] * 2,
            *[pltpu.VMEM((4 * width, 3 * width), bf16)] * 2,
            *[pltpu.VMEM((4, 3 * width, width), bf16)] * 2,
            *[pltpu.VMEM((4 * width, width), bf16)] * 2,
            dma((3, 3, 2)), dma((3, 3, 2)), dma((3, 4)), dma((3, 4)),
            dma((5,)), dma((5,)), dma((5,)), dma((5,)), dma((2, 5)), dma((2, 5)),
            dma((5,)), dma((3, 4)), dma((7,)),
        ],
        compiler_params=pltpu.CompilerParams(
            collective_id=0, has_side_effects=True, vmem_limit_bytes=63 * 1024 * 1024
        ),
        name="fused",
    )(sending, taking, heads, lower_fill, upper_fill, matrix, inverses.reshape(-1, width))


def kernel_body(matrix, row_order, inverses, lower_fill, upper_fill):
    nrows, width = matrix.shape[0], matrix.shape[2]
    p = lax.axis_index("prow")
    sending, taking, heads = tables(row_order, nrows, width, p)
    linear = matrix.reshape(nrows * width * 6, 128)
    out = fused(linear, sending, taking, heads, lower_fill, upper_fill, inverses, nrows, width)
    return out.reshape(matrix.shape)


def solution(mesh):
    in_specs = (P(None, "prow", None, None, "pcol", None), P(), P(), P(), P())
    out_specs = P(None, "prow", None, None, "pcol", None)
    fits = mesh.shape["prow"] == 4 and mesh.shape["pcol"] == 8
    return jax.shard_map(
        kernel_body if fits else body,
        mesh=mesh, in_specs=in_specs, out_specs=out_specs, check_vma=False,
    )
```

```python
import functools

import jax
import jax.numpy as jnp
from jax import lax
from jax.experimental import pallas as pl
from jax.experimental.pallas import tpu as pltpu
from jax.sharding import PartitionSpec as P


def mm(a, b):
    return jnp.dot(a, b, precision=lax.Precision.HIGH, preferred_element_type=jnp.float32)


def index_lists(row_order, rows, width, prows, here_row):
    local_rows = rows * width
    blocks = row_order.reshape(rows, prows, width)
    targets = lax.dynamic_index_in_dim(blocks, here_row, 1, keepdims=False).reshape(-1)
    local = jnp.arange(local_rows, dtype=jnp.int32)
    sending = (targets // width % prows) * local_rows + local
    by_source = jnp.transpose(blocks, (1, 0, 2)).reshape(-1)
    dest_local = by_source // width // prows * width + by_source % width
    mine = by_source // width % prows == here_row
    position = jnp.cumsum(mine.astype(jnp.int32)) - 1
    key = jnp.where(mine, dest_local * local_rows + position, local_rows * local_rows)
    both = jnp.concatenate([sending, prows * local_rows + key])
    both = lax.sort(both, is_stable=False)[: 2 * local_rows] % local_rows
    return both[:local_rows], both[local_rows:]


def keep_of(fill_row, panel, blocks):
    return (blocks > panel) & (fill_row[blocks] == 1)


def body(matrix, row_order, inverses, lower_fill, upper_fill):
    nrows = matrix.shape[0]
    width = matrix.shape[2]
    ncols = matrix.shape[3]
    prows = lax.axis_size("prow")
    pcols = lax.axis_size("pcol")
    p = lax.axis_index("prow")
    q = lax.axis_index("pcol")
    panels = inverses.shape[0]
    local_rows = nrows * width
    cols = ncols * width
    sending, taking = index_lists(row_order, nrows, width, prows, p)
    work = matrix.reshape(local_rows, cols)
    outgoing = work[sending].reshape(prows, local_rows // prows, cols)
    incoming = lax.all_to_all(outgoing, "prow", split_axis=0, concat_axis=0, tiled=True)
    work = incoming.reshape(local_rows, cols)[taking]
    tops = lax.all_gather(work[:width], "prow", axis=0, tiled=False)[:panels]
    tops = tops.reshape(panels * width, cols)
    column = jnp.concatenate([tops[:, :width], work[:, :width]], axis=0)
    ratio = pcols // panels
    pieces = column.reshape(ratio, -1, width)
    piece = jnp.where(q < panels, pieces[0], 0.0)
    for j in range(1, ratio):
        pairs = [(k, k + panels * j) for k in range(panels)]
        piece = piece + lax.ppermute(pieces[j], "pcol", pairs)
    every = lax.all_gather(piece, "pcol", axis=0, tiled=False)
    every = every.reshape(ratio, panels, piece.shape[0], width)
    columns = [every[:, k].reshape(column.shape) for k in range(panels)]
    row_blocks = jnp.concatenate(
        [jnp.arange(panels, dtype=jnp.int32), jnp.arange(nrows, dtype=jnp.int32) * prows + p]
    )
    col_blocks = jnp.arange(ncols, dtype=jnp.int32) * pcols + q
    corner = panels * width
    lowers, uppers = [], []
    mine = work[:, :width]
    for k in range(panels):
        here = columns[k]
        for m in range(k):
            keep = (upper_fill[m, k] == 1).astype(jnp.float32)
            part = here[m * width : (m + 1) * width] * keep
            here = here - mm(lowers[m], part)
        columns[k] = here
        row_keep = jnp.repeat(keep_of(lower_fill[k], k, row_blocks), width)[:, None]
        lower = jnp.where(row_keep, mm(here, inverses[k]), 0.0)
        lowers.append(lower)
        row = tops[k * width : (k + 1) * width]
        for m in range(k):
            row = row - mm(lower_rows(lowers[m], k, width), uppers[m])
        col_keep = jnp.repeat(keep_of(upper_fill[k], k, col_blocks), width)[None, :]
        uppers.append(jnp.where(col_keep, row, 0.0))
    left = jnp.concatenate([x[corner:] for x in lowers], axis=1)
    out = work - mm(left, jnp.concatenate(uppers, axis=0))
    row_ids = jnp.repeat(row_blocks[panels:], width)[:, None]
    first = out[:, :width]
    for k in range(panels):
        first = jnp.where((q == k) & (row_ids > k), lowers[k][corner:], first)
    out = out.at[:, :width].set(first)
    return out.reshape(nrows, 1, width, ncols, 1, width)


def lower_rows(lower, k, width):
    return lower[k * width : (k + 1) * width]


MESH = pl.DeviceIdType.MESH


def one_hot_sum(rows_of, lanes_of, values):
    groups = rows_of.shape[0]
    up = lax.broadcasted_iota(jnp.int32, (16, 128), 0)
    across = lax.broadcasted_iota(jnp.int32, (128, 128), 0)
    lefts, rights = [], []
    for g in range(groups):
        here = slice(g, g + 1)
        hit = up == rows_of[here]
        value = values[here]
        parts = [jnp.where(hit, value % 128, 0), jnp.where(hit, value // 128, 0)]
        lefts.append(jnp.concatenate(parts, axis=0).astype(jnp.float32).astype(jnp.bfloat16))
        rights.append((across == lanes_of[here]).astype(jnp.float32).astype(jnp.bfloat16))
    total = lax.dot_general(
        jnp.concatenate(lefts, axis=1), jnp.concatenate(rights, axis=1),
        (((1,), (1,)), ((), ())), preferred_element_type=jnp.float32,
    ).astype(jnp.int32)
    return total[:16] + 128 * total[16:]


def tables_kernel(nrows, width, order, out):
    p = lax.axis_index("prow")
    per = width // 128
    lines = nrows * per
    share = nrows * width // 4
    bf16 = jnp.bfloat16

    def dot(a, b):
        return jnp.dot(a, b, preferred_element_type=jnp.float32)

    by_source = [
        jnp.concatenate(
            [order[(r * 4 + s) * per : (r * 4 + s + 1) * per, :] for r in range(nrows)], axis=0
        )
        for s in range(4)
    ]
    targets = by_source[0] * (p == 0).astype(jnp.int32)
    for s in range(1, 4):
        targets = targets + by_source[s] * (p == s).astype(jnp.int32)
    arriving = jnp.concatenate(by_source, axis=0)
    leaving = jnp.concatenate([targets] * 4, axis=0)
    group = lax.broadcasted_iota(jnp.int32, (4 * lines, 128), 0) // lines
    mine = arriving // width % 4 == p
    theirs = leaving // width % 4 == group
    ranks = []
    up = lax.broadcasted_iota(jnp.int32, (4 * lines, 4 * lines), 0)
    along = lax.broadcasted_iota(jnp.int32, (4 * lines, 4 * lines), 1)
    same = up // lines == along // lines
    before = (same & (along < up)).astype(jnp.float32).astype(bf16)
    same = same.astype(jnp.float32).astype(bf16)
    upto = lax.broadcasted_iota(jnp.int32, (128, 128), 0)
    upto = upto <= lax.broadcasted_iota(jnp.int32, (128, 128), 1)
    upto = upto.astype(jnp.float32).astype(bf16)
    ones = jnp.ones((128, 128), bf16)
    for mask, where in ((mine, arriving), (theirs, leaving)):
        low = where < 4 * width
        first = (mask & low).astype(jnp.float32).astype(bf16)
        late = (mask & (where >= 4 * width)).astype(jnp.float32).astype(bf16)
        firsts = dot(first, upto) + dot(dot(before, first).astype(bf16), ones)
        lates = dot(late, upto) + dot(dot(before, late).astype(bf16), ones)
        count = dot(dot(same, first).astype(bf16), ones)
        rank = jnp.where(low, firsts, count + lates).astype(jnp.int32) - 1
        ranks.append(group * share + rank)
    dest = arriving // (4 * width) * width + arriving % width
    row = jnp.where(mine, dest // 128, 15)
    taking = one_hot_sum(row, dest % 128, ranks[0])
    spot = jnp.where(theirs, ranks[1], 0)
    spot = sum(spot[d * lines : (d + 1) * lines] for d in range(4))
    local = lax.broadcasted_iota(jnp.int32, (lines, 128), 0) * 128
    local = local + lax.broadcasted_iota(jnp.int32, (lines, 128), 1)
    sending = one_hot_sum(spot // 128, spot % 128, local)
    out[:16, :] = sending
    out[16:32, :] = taking
    source = sum((taking[:8] >= s * share).astype(jnp.int32) for s in (1, 2, 3))
    out[32:40, :] = taking[:8] - source * (share - width)


def tables(row_order, nrows, width):
    vmem = pl.BlockSpec(memory_space=pltpu.VMEM)
    return pl.pallas_call(
        functools.partial(tables_kernel, nrows, width),
        out_shape=jax.ShapeDtypeStruct((40, 128), jnp.int32),
        in_specs=[vmem], out_specs=vmem, name="tables",
    )(row_order.reshape(-1, 128)).reshape(-1)


SENDING, TAKING, HEADS = 0, 2048, 4096


def halves(x):
    high = x.astype(jnp.bfloat16)
    return high, (x - high.astype(jnp.float32)).astype(jnp.bfloat16)


def dot3(a, b):
    def dot(x, y):
        return jnp.dot(x, y, preferred_element_type=jnp.float32)

    return dot(a[0], b[0]) + dot(a[0], b[1]) + dot(a[1], b[0])


def fused_kernel(
    nrows, width, table, lower_fill, upper_fill, mat_in, inv, out, all2,
    mat, send, early0, early1, early2, all0, all1, mine2, work, tops, cols,
    lh, ll, uh, ul, ch, cl, ih, il,
    a2a_send, a2a_recv, g_send, g_recv, x_send, x_recv, y_send, y_recv, s_send, s_recv,
    keep_sem, join_sem, mat_sem,
):
    p = lax.axis_index("prow")
    q = lax.axis_index("pcol")
    side, across, core = q // 4, q // 2 % 2, q % 2
    xq = side * 4 + (1 - across) * 2 + core
    yq = (1 - side) * 4 + across * 2 + core
    sq = side * 4 + across * 2 + (1 - core)
    local_rows = nrows * width
    share = local_rows // 4
    top = 2 * width
    span6 = 6 * width
    late = 2 * (share - width)
    partner = p + 1 - 2 * (p % 2)
    others = [((p + 2) % 4, q), (3 - p, q), (partner, q)]
    early = (early0, early1, early2)
    full = (all0, all1, all2)

    load = pltpu.make_async_copy(mat_in, mat, mat_sem.at[6])
    load.start()
    barrier = pltpu.get_barrier_semaphore()
    for peer in others + [(p, xq), (p, yq), (p, sq)]:
        pl.semaphore_signal(barrier, inc=1, device_id=peer, device_id_type=MESH)
    pl.semaphore_wait(barrier, 6)
    load.wait()

    def remote(src, dst, send_sem, recv_sem, peer):
        return pltpu.make_async_remote_copy(
            src_ref=src, dst_ref=dst, send_sem=send_sem, recv_sem=recv_sem,
            device_id=peer, device_id_type=MESH,
        )

    def pick(dst, index_base, source, pitch, offset, count):
        unroll = 8

        def group(g, carry):
            for u in range(unroll):
                row = table[index_base + g * unroll + u]
                dst[pl.ds(g * (2 * unroll) + 2 * u, 2), :] = source[
                    pl.ds(row * pitch + offset, 2), :
                ]
            return carry

        lax.fori_loop(0, count // unroll, group, 0)

    def a2a(c, slot, part):
        if part == 0:
            src = send.at[c, slot, pl.ds(0, top)]
            dst = early[c].at[pl.ds(pl.multiple_of(p * top, 8), top)]
        else:
            src = send.at[c, slot, pl.ds(top, late)]
            dst = full[c].at[pl.ds(pl.multiple_of(p * (2 * share) + top, 8), late)]
        return remote(
            src, dst, a2a_send.at[c, slot, part], a2a_recv.at[c, slot, part], others[slot]
        )

    def pick_send(c, slot, part):
        base = others[slot][0] * share
        if part == 0:
            pick(send.at[c, slot, pl.ds(0, top)], SENDING + base, mat, 6, 2 * c, width)
        else:
            pick(
                send.at[c, slot, pl.ds(top, late)], SENDING + base + width, mat, 6, 2 * c,
                share - width,
            )

    def mine_copy():
        here = pl.ds(pl.multiple_of(p * (2 * share) + top, 8), late)
        return pltpu.make_async_copy(mine2, all2.at[here], mat_sem.at[7])

    def pick_mine(c):
        base = SENDING + p * share
        here = early[c].at[pl.ds(pl.multiple_of(p * top, 8), top)]
        pick(here, base, mat, 6, 2 * c, width)
        here = mine2
        if c < 2:
            here = full[c].at[pl.ds(pl.multiple_of(p * (2 * share) + top, 8), late)]
        pick(here, base + width, mat, 6, 2 * c, share - width)
        if c == 2:
            mine_copy().start()

    def start(c, slots, part):
        for slot in slots:
            a2a(c, slot, part).start()

    def join(c, s):
        return pltpu.make_async_copy(
            early[c].at[pl.ds(s * top, top)], full[c].at[pl.ds(s * 2 * share, top)],
            join_sem.at[c, s],
        )

    def top_of(c, owner):
        return tops.at[c, pl.ds(pl.multiple_of(owner * top, 8), top)]

    def early_in(c):
        for slot in range(3):
            a2a(c, slot, 0).wait_recv()
        for s in range(4):
            join(c, s).start()
        pick(top_of(c, p), HEADS, early[c], 2, 0, width)

    def late_in(c):
        for slot in range(3):
            a2a(c, slot, 1).wait_recv()
        for s in range(4):
            join(c, s).wait()

    cross = (2 - p // 2, q)
    inner = (p == 1) | (p == 2)
    outer = (p == 0) | (p == 3)
    far = 2 - 2 * (p // 2)

    def gather_copy(c, owner, sem, peer):
        here = top_of(c, owner)
        return remote(here, here, g_send.at[c, sem], g_recv.at[c, owner], peer)

    def gather_start(c):
        gather_copy(c, p, 1, cross).start()
        gather_copy(c, p, 0, (partner, q)).start()

    def gather_relay(c):
        @pl.when(inner)
        def _():
            for j in range(2):
                gather_copy(c, far + j, 2 + j, (partner, q)).wait_recv()
                gather_copy(c, far + j, 2 + j, (partner, q)).start()

    def gather_end(c):
        gather_copy(c, partner, 0, (partner, q)).wait_recv()

        @pl.when(outer)
        def _():
            for j in range(2):
                gather_copy(c, far + j, 2 + j, (partner, q)).wait_recv()

    def gather_sent(c):
        gather_copy(c, p, 1, cross).wait_send()
        gather_copy(c, p, 0, (partner, q)).wait_send()

        @pl.when(inner)
        def _():
            for j in range(2):
                gather_copy(c, far + j, 2 + j, (partner, q)).wait_send()

    straight = across * 2 + core
    crossed = (1 - across) * 2 + core
    runs = [(i, min(2, nrows - i)) for i in range(1, nrows, 2)] + [(0, 2), (2, 2)]
    owned = len(runs) - 2

    def place(block, piece):
        first, count = runs[piece]
        spot = first + 3 if piece < owned else first
        return cols.at[block, pl.ds(spot * top, count * top)]

    def first_source(piece):
        first, count = runs[piece]
        if piece < owned:
            return work.at[pl.ds(first * top, count * top)]
        return tops.at[0, pl.ds(first * top, count * top)]

    def to_x(src, piece):
        return remote(src, place(straight, piece), x_send.at[piece], x_recv.at[piece], (p, xq))

    def to_y(src, piece):
        return remote(src, place(straight, piece), y_send.at[piece], y_recv.at[piece], (p, yq))

    def to_s(src, kind, piece):
        block = (straight, crossed)[kind]
        return remote(
            src, place(block, piece), s_send.at[kind, piece], s_recv.at[kind, piece], (p, sq)
        )

    def keep_own(piece):
        return pltpu.make_async_copy(
            first_source(piece), place(straight, piece), keep_sem.at[piece]
        )

    def column_start(piece):
        @pl.when(side == 0)
        def _():
            src = first_source(piece)
            to_y(src, piece).start()
            to_x(src, piece).start()
            to_s(src, 0, piece).start()
            keep_own(piece).start()

    def column_pass(piece):
        @pl.when(side == 1)
        def _():
            here = place(straight, piece)
            to_y(here, piece).wait_recv()
            to_x(here, piece).start()
            to_s(here, 0, piece).start()

    def column_across(piece):
        here = place(crossed, piece)
        remote(here, here, x_send.at[piece], x_recv.at[piece], (p, xq)).wait_recv()
        to_s(here, 1, piece).start()

    def column_ready(piece):
        for kind in range(2):
            block = (straight, crossed)[kind]
            theirs = place(block + 1 - 2 * core, piece)
            remote(
                theirs, theirs, s_send.at[kind, piece], s_recv.at[kind, piece], (p, sq)
            ).wait_recv()

        @pl.when(side == 0)
        def _():
            keep_own(piece).wait()

    def column_sent(piece):
        for kind in range(2):
            block = (straight, crossed)[kind]
            to_s(place(block, piece), kind, piece).wait_send()
        to_x(place(straight, piece), piece).wait_send()

        @pl.when(side == 0)
        def _():
            to_y(place(straight, piece), piece).wait_send()

    def kept(fill, k, block):
        return jnp.where((block > k) & (fill[k, block] == 1), 1.0, 0.0)

    def column_tile(k, start):
        left = cols[k, pl.ds(2 * start, width, stride=2), :]
        right = cols[k, pl.ds(2 * start + 1, width, stride=2), :]
        return jnp.concatenate([left, right], axis=1)

    def lower_of(start, deep):
        rows = pl.ds(start, width)
        return lh[rows, :deep], ll[rows, :deep]

    def put_lower(start, k, h, keep):
        rows, here = pl.ds(start, width), slice(k * width, (k + 1) * width)
        inverse = ih[here, :], il[here, :]
        lh[rows, here], ll[rows, here] = halves(dot3(halves(h), inverse) * keep)

    def corner():
        for r in range(4):
            for k in range(4):
                if k >= r:
                    rows, there = pl.ds(r * width, width), slice(k * width, (k + 1) * width)
                    lh[rows, there] = jnp.zeros((width, width), jnp.bfloat16)
                    ll[rows, there] = jnp.zeros((width, width), jnp.bfloat16)
                if k == r:
                    continue
                h = column_tile(k, r * width)
                deep = min(r, k) * width
                if deep:
                    h = h - dot3(lower_of(r * width, deep), (ch[k, :deep, :], cl[k, :deep, :]))
                if k < r:
                    put_lower(r * width, k, h, kept(lower_fill, k, r))
                else:
                    here = slice(r * width, (r + 1) * width)
                    ch[k, here, :], cl[k, here, :] = halves(h * kept(upper_fill, r, k))

    def panels(piece):
        for k in range(4):
            for i in range(runs[piece][0], sum(runs[piece])):
                begin = (3 + i) * width
                h = column_tile(k, begin)
                deep = k * width
                if deep:
                    h = h - dot3(lower_of(begin, deep), (ch[k, :deep, :], cl[k, :deep, :]))
                put_lower(begin, k, h, kept(lower_fill, k, i * 4 + p))

    def upper(c):
        span = slice(c * width, (c + 1) * width)
        for r in range(4):
            left = tops[c, pl.ds(2 * r * width, width, stride=2), :]
            right = tops[c, pl.ds(2 * r * width + 1, width, stride=2), :]
            u = jnp.concatenate([left, right], axis=1)
            deep = r * width
            if deep:
                u = u - dot3(lower_of(r * width, deep), (uh[:deep, span], ul[:deep, span]))
            here = slice(r * width, (r + 1) * width)
            uh[here, span], ul[here, span] = halves(u * kept(upper_fill, r, c * 8 + q))

    def update(c):
        span = slice(c * width, (c + 1) * width)

        def tile(i, spot):
            begin = pl.multiple_of(spot * width, width)
            value = dot3(lower_of(begin, 4 * width), (uh[:, span], ul[:, span]))
            if c == 0:
                at = pl.multiple_of(i * (2 * width), 8)
                old = jnp.concatenate(
                    [
                        work[pl.ds(at, width, stride=2), :],
                        work[pl.ds(at + 1, width, stride=2), :],
                    ],
                    axis=1,
                )
                value = old - value
                for k in range(4):
                    here = slice(k * width, (k + 1) * width)
                    rows = pl.ds(begin, width)
                    low = lh[rows, here].astype(jnp.float32) + ll[rows, here].astype(jnp.float32)
                    value = jnp.where((q == k) & (i * 4 + p > k), low, value)
            for half in range(2):
                part = value[:, half * 128 : (half + 1) * 128]
                rows = pl.ds(i * span6 + 2 * c + half, width, stride=6)
                if c == 1:
                    part = mat[rows, :] - part
                mat[rows, :] = part

        def step(i, carry):
            tile(i, 3 + i)
            return carry

        tile(0, p)
        lax.fori_loop(1, nrows, step, 0)

    def take(c):
        def group(g, carry):
            for u in range(8):
                row = table[TAKING + g * 8 + u]
                here = pl.ds(g * 48 + u * 6 + 2 * c, 2)
                mat[here, :] = full[c][pl.ds(row * 2, 2), :]
            return carry

        lax.fori_loop(0, local_rows // 8, group, 0)

    def leave(i):
        rows = pl.ds(i * span6, span6)
        return pltpu.make_async_copy(mat.at[rows], out.at[rows], mat_sem.at[i])

    for slot in range(3):
        pick_send(0, slot, 0)
        start(0, (slot,), 0)
    for slot in range(3):
        pick_send(0, slot, 1)
        start(0, (slot,), 1)
    pick_mine(0)
    for c in (1, 2):
        for part in range(2):
            for slot in range(3):
                pick_send(c, slot, part)
        pick_mine(c)
    ih[...], il[...] = halves(inv[...])
    early_in(0)
    gather_start(0)
    start(1, (0, 1), 0)
    start(1, (0, 1), 1)
    late_in(0)
    pick(work, TAKING, all0, 2, 0, local_rows)
    column_start(0)
    gather_relay(0)
    start(1, (2,), 0)
    start(1, (2,), 1)
    gather_end(0)
    column_start(3)
    column_start(4)
    column_start(1)
    column_start(2)
    column_pass(0)
    column_across(0)
    column_pass(3)
    early_in(1)
    gather_start(1)
    start(2, (0, 1), 0)
    start(2, (0,), 1)
    column_across(3)
    column_pass(4)
    late_in(1)
    take(1)
    column_across(4)
    column_pass(1)
    gather_relay(1)
    start(2, (2,), 0)
    column_ready(3)
    column_ready(4)
    corner()
    column_pass(2)
    column_ready(0)
    panels(0)
    column_across(1)
    column_across(2)
    column_ready(1)
    panels(1)
    column_ready(2)
    panels(2)
    gather_end(1)
    upper(0)
    upper(1)
    update(0)
    early_in(2)
    gather_start(2)
    start(2, (1,), 1)
    update(1)
    gather_relay(2)
    start(2, (2,), 1)
    gather_end(2)
    upper(2)
    update(2)
    for i in range(nrows):
        leave(i).start()
    mine_copy().wait()
    late_in(2)
    for c in range(3):
        gather_sent(c)
        for slot in range(3):
            for part in range(2):
                a2a(c, slot, part).wait_send()
    for piece in range(owned + 2):
        column_sent(piece)
    for i in range(nrows):
        leave(i).wait()


def fused(matrix, table, lower_fill, upper_fill, inverses, nrows, width):
    local_rows = nrows * width
    share = local_rows // 4
    dma = pltpu.SemaphoreType.DMA
    vmem = pl.BlockSpec(memory_space=pltpu.VMEM)
    smem = pl.BlockSpec(memory_space=pltpu.SMEM)
    hbm = pl.BlockSpec(memory_space=pl.ANY)
    f32, bf16 = jnp.float32, jnp.bfloat16
    tiles = 3 + nrows
    return pl.pallas_call(
        functools.partial(fused_kernel, nrows, width),
        out_shape=(
            jax.ShapeDtypeStruct((6 * local_rows, 128), f32),
            jax.ShapeDtypeStruct((2 * local_rows, 128), f32),
        ),
        in_specs=[smem] * 3 + [hbm, vmem],
        out_specs=(hbm, hbm),
        scratch_shapes=[
            pltpu.VMEM((6 * local_rows, 128), f32),
            pltpu.VMEM((3, 3, 2 * share, 128), f32),
            *[pltpu.VMEM((8 * width, 128), f32)] * 3,
            *[pltpu.VMEM((2 * local_rows, 128), f32)] * 2,
            pltpu.VMEM((2 * (share - width), 128), f32),
            pltpu.VMEM((2 * local_rows, 128), f32),
            pltpu.VMEM((3, 8 * width, 128), f32),
            pltpu.VMEM((4, 2 * tiles * width, 128), f32),
            *[pltpu.VMEM((tiles * width, 4 * width), bf16)] * 2,
            *[pltpu.VMEM((4 * width, 3 * width), bf16)] * 2,
            *[pltpu.VMEM((4, 3 * width, width), bf16)] * 2,
            *[pltpu.VMEM((4 * width, width), bf16)] * 2,
            dma((3, 3, 2)), dma((3, 3, 2)), dma((3, 4)), dma((3, 4)),
            dma((5,)), dma((5,)), dma((5,)), dma((5,)), dma((2, 5)), dma((2, 5)),
            dma((5,)), dma((3, 4)), dma((8,)),
        ],
        compiler_params=pltpu.CompilerParams(
            collective_id=0, has_side_effects=True, vmem_limit_bytes=63 * 1024 * 1024
        ),
        name="fused",
    )(table, lower_fill, upper_fill, matrix, inverses.reshape(-1, width))


def last_kernel(nrows, width, table, part, rows_in, out, mat, rows, sems):
    span = 6 * width

    def load(i):
        here = pl.ds(i * span, span)
        return pltpu.make_async_copy(part.at[here], mat.at[here], sems.at[0, i])

    def store(i):
        here = pl.ds(i * span, span)
        return pltpu.make_async_copy(mat.at[here], out.at[here], sems.at[1, i])

    incoming = pltpu.make_async_copy(rows_in, rows, sems.at[0, nrows])
    incoming.start()
    for i in range(nrows):
        load(i).start()
    incoming.wait()
    for i in range(nrows):
        load(i).wait()

        def group(g, carry):
            for u in range(8):
                row = table[TAKING + i * width + g * 8 + u]
                here = pl.ds(i * span + g * 48 + u * 6 + 4, 2)
                mat[here, :] = rows[pl.ds(row * 2, 2), :] - mat[here, :]
            return carry

        lax.fori_loop(0, width // 8, group, 0)
        store(i).start()
    for i in range(nrows):
        store(i).wait()


def last(table, part, rows, nrows, width):
    hbm = pl.BlockSpec(memory_space=pl.ANY)
    return pl.pallas_call(
        functools.partial(last_kernel, nrows, width),
        out_shape=jax.ShapeDtypeStruct(part.shape, part.dtype),
        in_specs=[pl.BlockSpec(memory_space=pltpu.SMEM), hbm, hbm],
        out_specs=hbm,
        scratch_shapes=[
            pltpu.VMEM(part.shape, part.dtype),
            pltpu.VMEM(rows.shape, rows.dtype),
            pltpu.SemaphoreType.DMA((2, nrows + 1)),
        ],
        compiler_params=pltpu.CompilerParams(vmem_limit_bytes=60 * 1024 * 1024),
        name="last",
    )(table, part, rows)


def kernel_body(matrix, row_order, inverses, lower_fill, upper_fill):
    nrows, width = matrix.shape[0], matrix.shape[2]
    table = tables(row_order, nrows, width)
    linear = matrix.reshape(nrows * width * 6, 128)
    part, rows = fused(linear, table, lower_fill, upper_fill, inverses, nrows, width)
    return last(table, part, rows, nrows, width).reshape(matrix.shape)


def solution(mesh):
    in_specs = (P(None, "prow", None, None, "pcol", None), P(), P(), P(), P())
    out_specs = P(None, "prow", None, None, "pcol", None)
    fits = mesh.shape["prow"] == 4 and mesh.shape["pcol"] == 8
    return jax.shard_map(
        kernel_body if fits else body,
        mesh=mesh, in_specs=in_specs, out_specs=out_specs, check_vma=False,
    )
```
